32 devices in a mesh: dp: 4 (over z), expert: 8 (over y, x, core).
Axes of the slice: x: 2, y: 2, z: 4, core: 2. Of those that a mesh axis runs over, the one named last changes fastest.
Arguments:
- tokens: bfloat16 [4096, 2048], P(('dp', 'expert')), may hold values from -6 to 6
- routes: int32 [4096, 8], P(('dp', 'expert')), may hold values from 0 to 31, all different within a row; in each aligned block of 128 rows (0 to 127, 128 to 255, ...) at most 38 rows name the same one
- prefix_len: int32 [4], P('dp'), may hold values from 102 to 512
- query_weight: bfloat16 [2048, 4096], P('dp', 'expert'), may hold values from -0.125 to 0.125
- key_matrix: bfloat16 [2048, 512], P('dp', 'expert'), may hold values from -0.125 to 0.125
- value_matrix: bfloat16 [2048, 512], P('dp', 'expert'), may hold values from -0.125 to 0.125
- out_weight: bfloat16 [4096, 2048], P('dp', 'expert'), may hold values from -2 to 2
- router_weight: bfloat16 [2048, 32], P('dp', 'expert'), may hold values from -0.0625 to 0.0625
- attention_gain: float32 [2048], replicated, may hold values from 0.25 to 1.75
- mixture_gain: float32 [2048], replicated, may hold values from 0.25 to 1.75
- query_gain: float32 [128], replicated, may hold values from 0.25 to 1.75
- key_norm_gain: float32 [128], replicated, may hold values from 0.25 to 1.75
- expert_gate: bfloat16 [32, 2048, 768], P(('dp', 'expert')), may hold values from -0.125 to 0.125
- expert_up: bfloat16 [32, 2048, 768], P(('dp', 'expert')), may hold values from -0.125 to 0.125
- expert_down: bfloat16 [32, 768, 2048], P(('dp', 'expert')), may hold values from -0.875 to 0.875
- cotangent: bfloat16 [4096, 2048], P(('dp', 'expert')), may hold values from -6 to 6
Outputs:
- layer_out: bfloat16 [4096, 2048], P(('dp', 'expert'))
- input_grad: float32 [4096, 2048], P(('dp', 'expert'))
- query_weight_grad: float32 [2048, 4096], P('dp', 'expert')
- key_weight_grad: float32 [2048, 512], P('dp', 'expert')
- value_weight_grad: float32 [2048, 512], P('dp', 'expert')
- out_weight_grad: float32 [4096, 2048], P('dp', 'expert')
- router_grad: float32 [2048, 32], P('dp', 'expert')
- attention_gain_grad: float32 [2048], replicated
- mixture_gain_grad: float32 [2048], replicated
- query_gain_grad: float32 [128], replicated
- key_gain_grad: float32 [128], replicated
- expert_gate_grad: float32 [32, 2048, 768], P(('dp', 'expert'))
- expert_up_grad: float32 [32, 2048, 768], P(('dp', 'expert'))
- expert_down_grad: float32 [32, 768, 2048], P(('dp', 'expert'))
The draws below stay inside these ranges and needn't reach their ends.
Inputs may be any that keep to these rules, and one draw needn't show every extreme that they name: `routes`: each row names 8 different experts. In the rows of one device no expert is named more than 38 times, and in every draw the rows of some device name some expert exactly 38 times.
All inputs are finite; a program needn't handle non-finite values.
Results may differ from the reference program's by a relative error of at most 0.025.
Values may be sent and summed in bfloat16 or wider, within the bound.
No kernel may reach another device: no remote copies, remote signals or barrier semaphores. Data moves between devices by JAX's collectives and lax.ppermute only.
A program may use at most 256 MiB of HBM per device.

```python
import math
import jax
import jax.numpy as jnp
import numpy as np
from jax import lax

MODEL_WIDTH = 2048
QUERY_HEADS = 32
KEY_VALUE_HEADS = 4
HEAD_SIZE = 128
FFE = 768
TOP = 8
TOK_DEV = 128
EXPERTS = 32
CAP = 38
SEQUENCE_LENGTH = 1024
SEQUENCE_COUNT = 4
TOKENS = 4096
N_DP = 4
N_EXPERT = 8


def with_ends(drawn, own_key, smallest, high):
    place = [jax.random.randint(jax.random.fold_in(own_key, axis), (), 0, length) for axis, length in enumerate(drawn.shape)]
    longest = drawn.shape.index(max(drawn.shape))
    beside = place[:longest] + [(place[longest] + 1) % drawn.shape[longest]] + place[longest + 1:]
    return drawn.at[tuple(place)].set(smallest).at[tuple(beside)].set(high)


def level_of(rng, shape, shards, smallest, largest):
    factor_of = 1.0
    for axis_at, shards_of in shards:
        steps = jax.random.uniform(jax.random.fold_in(jax.random.fold_in(rng, 6), axis_at), (shards_of,), jnp.float32, smallest / len(shards), largest / len(shards))
        factor_of = factor_of * jnp.repeat(jnp.exp(steps), shape[axis_at] // shards_of).reshape((-1,) + (1,) * (len(shape) - 1 - axis_at))
    return factor_of


def assign_block(stream_key, own, number, rows, number_of, top, bound, slope):
    sequence = jax.random.permutation(stream_key, number_of)
    crowded, common = shares(number_of, rows * top, bound, slope, True), shares(number_of, rows * top, bound, slope, False)
    places = jnp.arange(number_of)

    def named(tallies, rotation):
        used = int((tallies > 0).sum())
        fixed = max(1, used // 4)
        passed = fixed + (places - fixed + rotation * (used - fixed)) % max(1, number_of - fixed)
        return jnp.zeros((number_of,), jnp.int32).at[sequence[jnp.where(places < fixed, places, passed)]].set(jnp.asarray(tallies, jnp.int32))

    tallies = jnp.where(number % 4 == 0, named(crowded, number // 4), named(common, number - number // 4 - 1))
    mixed = jax.random.permutation(jax.random.fold_in(own, 3), number_of)
    donor, receiver = mixed[0:number_of // 2 * 2:2], mixed[1:number_of // 2 * 2:2]
    room = jnp.minimum(tallies[donor] - 1, bound - tallies[receiver]) // 2
    room = jnp.where((donor == sequence[0]) | (receiver == sequence[0]) | (tallies[receiver] == 0), 0, jnp.maximum(room, 0))
    passed = jax.random.randint(jax.random.fold_in(own, 4), (number_of // 2,), 0, 1 << 20) % (room + 1)
    tallies = tallies.at[donor].add(-passed).at[receiver].add(passed)
    items = jnp.searchsorted(jnp.cumsum(tallies), jnp.arange(rows * top), side="right").astype(jnp.int32)
    grid = items.reshape(top, rows).T
    grid = grid[jax.random.permutation(jax.random.fold_in(own, 1), rows)]
    rotation = jax.random.randint(jax.random.fold_in(own, 2), (rows, 1), 0, top)
    return jnp.take_along_axis(grid, (jnp.arange(top)[None, :] + rotation) % top, axis=1)


def shares(amount, total, bound, lean, full):
    weights = [(1 << 20) // math.isqrt(rank ** lean) + 1 for rank in range(1, amount + 1)]
    largest = bound if full else min(bound, max(-(-total // amount), total * weights[0] // sum(weights)))
    least = 1 if total - largest >= amount - 1 else 0
    holding, rest = [largest] + [least] * (amount - 1), total - largest - least * (amount - 1)
    while rest > 0:
        movable = [i for i in range(1, amount) if holding[i] < largest] or [i for i in range(1, amount) if holding[i] < bound]
        mass, left = sum([weights[i] for i in movable]), rest
        for i in movable:
            more = min(bound - holding[i], max(1, left * weights[i] // mass), rest)
            holding[i] = holding[i] + more
            rest = rest - more
    return np.array(holding)


def gaussian(rng, shape, width, limit, split=(), kind=jnp.bfloat16):
    array = jax.random.normal(rng, shape, jnp.float32) * width
    if len(split) > 0:
        array = level_of(rng, shape, split, -0.22, 0.18) * array
    return jnp.clip(array, min=-limit, max=limit).astype(kind)


def setup_inputs(seed: int = 0) -> dict:
    splits = jax.random.split(jax.random.key(seed), 17)
    tokens = gaussian(splits[0], (TOKENS, MODEL_WIDTH), 1.0, 6.0, ((0, 32),))
    routes_keys = jax.random.split(jax.random.fold_in(splits[1], 1), TOKENS // TOK_DEV)
    routes_turns = jax.random.permutation(jax.random.fold_in(splits[1], 3), TOKENS // TOK_DEV)
    routes = jax.vmap(lambda own, number: assign_block(jax.random.fold_in(splits[1], 2), own, number, TOK_DEV, EXPERTS, TOP, CAP, 1))(routes_keys, routes_turns).reshape((TOKENS, TOP))
    prefix_len = with_ends(jax.random.randint(splits[2], (SEQUENCE_COUNT,), SEQUENCE_LENGTH // 10, SEQUENCE_LENGTH // 2 + 1), jax.random.fold_in(splits[2], 1), SEQUENCE_LENGTH // 10, (SEQUENCE_LENGTH // 2 + 1) - 1).astype(jnp.int32)
    query_weight = gaussian(splits[3], (MODEL_WIDTH, QUERY_HEADS * HEAD_SIZE), MODEL_WIDTH ** -0.5, 0.125, ((0, 4), (1, 8)))
    key_matrix = gaussian(splits[4], (MODEL_WIDTH, KEY_VALUE_HEADS * HEAD_SIZE), MODEL_WIDTH ** -0.5, 0.125, ((0, 4), (1, 8)))
    value_matrix = gaussian(splits[5], (MODEL_WIDTH, KEY_VALUE_HEADS * HEAD_SIZE), MODEL_WIDTH ** -0.5, 0.125, ((0, 4), (1, 8)))
    out_weight = gaussian(splits[6], (QUERY_HEADS * HEAD_SIZE, MODEL_WIDTH), (max(8, QUERY_HEADS * HEAD_SIZE // 512)) ** -0.5, 2.0, ((0, 4), (1, 8)))
    router_weight = gaussian(splits[7], (MODEL_WIDTH, EXPERTS), (MODEL_WIDTH * 4) ** -0.5, 0.0625, ((0, 4), (1, 8)))
    attention_gain = jnp.clip(1.0 + 0.15 * jax.random.normal(splits[8], (MODEL_WIDTH,), jnp.float32), 0.25, 1.75)
    mixture_gain = jnp.clip(1.0 + 0.15 * jax.random.normal(splits[9], (MODEL_WIDTH,), jnp.float32), 0.25, 1.75)
    query_gain = jnp.clip(1.0 + 0.15 * jax.random.normal(splits[10], (HEAD_SIZE,), jnp.float32), 0.25, 1.75)
    key_norm_gain = jnp.clip(1.0 + 0.15 * jax.random.normal(splits[11], (HEAD_SIZE,), jnp.float32), 0.25, 1.75)
    expert_gate = gaussian(splits[12], (EXPERTS, MODEL_WIDTH, FFE), MODEL_WIDTH ** -0.5, 0.125, ((0, 32),))
    expert_up = gaussian(splits[13], (EXPERTS, MODEL_WIDTH, FFE), MODEL_WIDTH ** -0.5, 0.125, ((0, 32),))
    expert_down = gaussian(splits[14], (EXPERTS, FFE, MODEL_WIDTH), (FFE // 16) ** -0.5, 0.875, ((0, 32),))
    cotangent = gaussian(splits[15], (TOKENS, MODEL_WIDTH), 1.0, 6.0, ((0, 32),))
    return dict(tokens=tokens, routes=routes, prefix_len=prefix_len, query_weight=query_weight, key_matrix=key_matrix, value_matrix=value_matrix, out_weight=out_weight, router_weight=router_weight, attention_gain=attention_gain, mixture_gain=mixture_gain, query_gain=query_gain, key_norm_gain=key_norm_gain, expert_gate=expert_gate, expert_up=expert_up, expert_down=expert_down, cotangent=cotangent)


EPS = 1e-06
ROTARY_BASE = 1000000.0
VERY_NEGATIVE = -1e+30
PRECISE = lax.Precision.HIGHEST

@jax.custom_vjp
def narrow_precision(v):
    return lax.optimization_barrier(v.astype(jnp.bfloat16)).astype(jnp.float32)

@jax.custom_vjp
def low_back(v):
    return v

def low_keep(v):
    return (narrow_precision(v), None)

def low_pass(kept, grad):
    return (grad,)

def back_keep(v):
    return (v, None)

def back_low(kept, grad):
    return (narrow_precision(grad),)
narrow_precision.defvjp(low_keep, low_pass)
low_back.defvjp(back_keep, back_low)

def head_normalize(source, gain_row):
    scaling = lax.rsqrt(lax.optimization_barrier(jnp.mean(source * source, axis=-1, keepdims=True)) + EPS)
    return source * scaling * gain_row

def rotary(span_length):
    half_dim = HEAD_SIZE // 2
    frequency = jnp.power(ROTARY_BASE, -jnp.arange(half_dim, dtype=jnp.float32) * 2.0 / HEAD_SIZE)
    places = jnp.arange(span_length, dtype=jnp.int32).astype(jnp.float32)
    angles = places[:, None] * frequency[None, :]
    cosine_lookup = jnp.concatenate([jnp.cos(angles), jnp.cos(angles)], axis=-1)[:, None, :]
    sine_lookup = jnp.concatenate([jnp.sin(angles), jnp.sin(angles)], axis=-1)[:, None, :]
    return (cosine_lookup, sine_lookup)

def rotary_apply(source, cosine_lookup, sine_lookup):
    half_dim = source.shape[-1] // 2
    front_half = source[..., :half_dim]
    back_half = source[..., half_dim:]
    return source * cosine_lookup + jnp.concatenate([-back_half, front_half], axis=-1) * sine_lookup

def attend_sequence(query_sequence, key_sequence, value_sequence, prefix):
    span_length = key_sequence.shape[0]
    rows_per_block = TOK_DEV
    count_of_blocks = span_length // rows_per_block
    query_tiles = query_sequence.reshape(count_of_blocks, rows_per_block, KEY_VALUE_HEADS, QUERY_HEADS // KEY_VALUE_HEADS, HEAD_SIZE)
    starts = jnp.arange(count_of_blocks, dtype=jnp.int32) * rows_per_block
    key_place = jnp.arange(span_length, dtype=jnp.int32)

    def one_block(packed):
        query_block, block_start = packed
        scores = low_back(jnp.einsum('thgd,shd->hgts', query_block, key_sequence, precision=PRECISE) * HEAD_SIZE ** (-0.5))
        query_place = block_start + jnp.arange(rows_per_block, dtype=jnp.int32)
        allowed = (key_place[None, :] <= query_place[:, None]) | (key_place[None, :] < prefix)
        weights_low = narrow_precision(jax.nn.softmax(jnp.where(allowed, scores, VERY_NEGATIVE), axis=-1))
        return jnp.einsum('hgts,shd->thgd', weights_low, value_sequence, precision=PRECISE)
    block_list = lax.map(jax.checkpoint(one_block), (query_tiles, starts))
    return block_list.reshape(span_length, KEY_VALUE_HEADS, QUERY_HEADS // KEY_VALUE_HEADS, HEAD_SIZE)

def dispatch_slots(routes):
    devices = N_DP * N_EXPERT
    per_device = routes.reshape(devices, TOK_DEV * TOP)
    one_hot = (per_device[:, :, None] == jnp.arange(EXPERTS, dtype=jnp.int32)[None, None, :]).astype(jnp.int32)
    slot_rank = lax.optimization_barrier(jnp.sum(jnp.cumsum(one_hot, axis=1) * one_hot, axis=2)) - 1
    sources = jnp.arange(devices, dtype=jnp.int32)[:, None]
    return (per_device * (devices * CAP) + sources * CAP + slot_rank).reshape(-1)

def expert_rows(packed):
    rows_in, gate_matrix, up_matrix, down_matrix = packed
    gate_value = low_back(jnp.dot(rows_in, gate_matrix, precision=PRECISE))
    up_value = low_back(jnp.dot(rows_in, up_matrix, precision=PRECISE))
    activated = narrow_precision(jax.nn.silu(gate_value) * up_value)
    return narrow_precision(low_back(jnp.dot(activated, down_matrix, precision=PRECISE)))

def layer(tokens, query_weight, key_matrix, value_matrix, out_weight, router_weight, attention_gain, mixture_gain, query_gain, key_norm_gain, expert_gate, expert_up, expert_down, routes, prefix_len):
    head_groups = QUERY_HEADS // KEY_VALUE_HEADS
    devices = N_DP * N_EXPERT
    normed = narrow_precision(head_normalize(tokens, attention_gain))
    query_raw = low_back(jnp.dot(normed, query_weight, precision=PRECISE))
    key_unnormed = low_back(jnp.dot(normed, key_matrix, precision=PRECISE))
    value_narrow = narrow_precision(low_back(jnp.dot(normed, value_matrix, precision=PRECISE)))
    cosine_lookup, sine_lookup = rotary(SEQUENCE_LENGTH)
    query_sequence = head_normalize(query_raw.reshape(SEQUENCE_COUNT, SEQUENCE_LENGTH, QUERY_HEADS, HEAD_SIZE), query_gain)
    query_narrow = narrow_precision(rotary_apply(query_sequence, cosine_lookup, sine_lookup)).reshape(SEQUENCE_COUNT, SEQUENCE_LENGTH, KEY_VALUE_HEADS, head_groups, HEAD_SIZE)
    key_sequence = head_normalize(key_unnormed.reshape(SEQUENCE_COUNT, SEQUENCE_LENGTH, KEY_VALUE_HEADS, HEAD_SIZE), key_norm_gain)
    key_low = narrow_precision(rotary_apply(key_sequence, cosine_lookup, sine_lookup))
    value_sequence = value_narrow.reshape(SEQUENCE_COUNT, SEQUENCE_LENGTH, KEY_VALUE_HEADS, HEAD_SIZE)
    attended = lax.map(lambda packed: attend_sequence(packed[0], packed[1], packed[2], packed[3]), (query_narrow, key_low, value_sequence, prefix_len))
    attended_low = narrow_precision(low_back(attended.reshape(TOKENS, QUERY_HEADS * HEAD_SIZE)))
    after_attn = tokens + low_back(jnp.dot(attended_low, out_weight, precision=PRECISE))
    mixed_low = narrow_precision(head_normalize(after_attn, mixture_gain))
    logits = low_back(jnp.dot(mixed_low, router_weight, precision=PRECISE))
    chosen = jnp.take_along_axis(logits, routes, axis=1)
    route_weight = jax.nn.softmax(chosen, axis=-1)
    slot_index = dispatch_slots(routes)
    sent_rows = low_back(jnp.repeat(mixed_low, TOP, axis=0))
    buffer = jnp.zeros((EXPERTS * devices * CAP, MODEL_WIDTH), jnp.float32).at[slot_index].set(sent_rows)
    buffer = buffer.reshape(EXPERTS, devices * CAP, MODEL_WIDTH)
    produced = lax.map(jax.checkpoint(expert_rows), (buffer, expert_gate, expert_up, expert_down))
    picked = produced.reshape(EXPERTS * devices * CAP, MODEL_WIDTH)[slot_index].reshape(TOKENS, TOP, MODEL_WIDTH)
    return after_attn + lax.optimization_barrier(jnp.sum(picked * route_weight[:, :, None], axis=1))

def reference(tokens, routes, prefix_len, query_weight, key_matrix, value_matrix, out_weight, router_weight, attention_gain, mixture_gain, query_gain, key_norm_gain, expert_gate, expert_up, expert_down, cotangent):
    floats = (tokens.astype(jnp.float32), query_weight.astype(jnp.float32), key_matrix.astype(jnp.float32), value_matrix.astype(jnp.float32), out_weight.astype(jnp.float32), router_weight.astype(jnp.float32), attention_gain.astype(jnp.float32), mixture_gain.astype(jnp.float32), query_gain.astype(jnp.float32), key_norm_gain.astype(jnp.float32), expert_gate.astype(jnp.float32), expert_up.astype(jnp.float32), expert_down.astype(jnp.float32))

    def forward(*params):
        return layer(*params, routes, prefix_len)
    result, pullback = jax.vjp(forward, *floats)
    grads = pullback(cotangent.astype(jnp.float32))
    return (result.astype(jnp.bfloat16), grads[0], grads[1], grads[2], grads[3], grads[4], grads[5], grads[6], grads[7], grads[8], grads[9], grads[10], grads[11], grads[12])
```

```python
import jax
import jax.numpy as jnp
from jax import lax
from jax.experimental import pallas as pl
from jax.experimental.pallas import tpu as pltpu
from jax.sharding import PartitionSpec as P

QUERY_HEADS = 32
KEY_VALUE_HEADS = 4
HEAD_SIZE = 128
TOP = 8
EPS = 1e-06
ROTARY_BASE = 1000000.0
VERY_NEGATIVE = -1e30
SCALE = HEAD_SIZE ** (-0.5)
F32 = jnp.float32
BF16 = jnp.bfloat16
BOTH = ("dp", "expert")


def dot(a, b, dims=((1,), (0,))):
    return lax.dot_general(a, b, (dims, ((), ())), preferred_element_type=F32)


def scale_of(u):
    return lax.rsqrt(jnp.mean(u * u, axis=-1, keepdims=True) + EPS)


def norm_back(upstream, unit, scaling, gain):
    weighted = upstream * gain
    return scaling * (weighted - unit * jnp.mean(weighted * unit, axis=-1, keepdims=True))


def rotary_tables(span):
    half = HEAD_SIZE // 2
    frequency = jnp.power(ROTARY_BASE, -jnp.arange(half, dtype=F32) * 2.0 / HEAD_SIZE)
    angles = jnp.arange(span, dtype=jnp.int32).astype(F32)[:, None] * frequency[None, :]
    cosine, sine = jnp.cos(angles), jnp.sin(angles)
    return jnp.concatenate([cosine, cosine], axis=-1), jnp.concatenate([-sine, sine], axis=-1)


def rope(u, cosine, sine):
    return u * cosine + pltpu.roll(u, HEAD_SIZE // 2, 1) * sine


def rope_back(g, cosine, sine):
    return g * cosine - pltpu.roll(g, HEAD_SIZE // 2, 1) * sine


def block_spans(span):
    rows = min(256, span)
    return [(at, rows, max(at + rows, span // 2)) for at in range(0, span, rows)]


def allowed_of(at, rows, keys, prefix):
    key_place = lax.broadcasted_iota(jnp.int32, (keys, rows), 0)
    query_place = at + lax.broadcasted_iota(jnp.int32, (keys, rows), 1)
    return (key_place <= query_place) | (key_place < prefix)


def attend_kernel(
    prefix_ref, q_ref, k_ref, v_ref, qgain_ref, kgain_ref, cos_ref, sin_ref,
    out_ref, lse_ref, qlow_ref, klow, vturned,
):
    span = q_ref.shape[0]
    prefix = prefix_ref[0]

    @pl.when(pl.program_id(0) == 0)
    def _():
        k = k_ref[...]
        klow[...] = rope(k * scale_of(k) * kgain_ref[...], cos_ref[...], sin_ref[...]).astype(BF16)
        vturned[...] = v_ref[...].T.astype(BF16)

    q = q_ref[...]
    qlow_ref[...] = rope(q * scale_of(q) * qgain_ref[...], cos_ref[...], sin_ref[...]).astype(BF16)
    for at, rows, keys in block_spans(span):
        qlow = qlow_ref[at : at + rows, :]
        scores = dot(klow[:keys, :], qlow, ((1,), (1,))) * SCALE
        scores = jnp.where(allowed_of(at, rows, keys, prefix), scores, VERY_NEGATIVE)
        high = jnp.max(scores, axis=0, keepdims=True)
        weights = jnp.exp(scores - high)
        total = jnp.sum(weights, axis=0, keepdims=True)
        weights_low = (weights * (1.0 / total)).astype(BF16)
        out = dot(vturned[:, :keys], weights_low)
        out_ref[at : at + rows, :] = out.T.astype(BF16)
        lse_ref[0, :, at : at + rows] = high + jnp.log(total)


def attend(prefix, qkv, heads, qgain, kgain, cosine, sine):
    span = qkv.shape[0]
    whole = lambda h: (0, 0)
    column = lambda index: pl.BlockSpec((span, HEAD_SIZE), index)
    keys = sum(rows * keys for _, rows, keys in block_spans(span))
    return pl.pallas_call(
        attend_kernel,
        grid=(heads,),
        in_specs=[
            pl.BlockSpec(memory_space=pltpu.SMEM),
            column(lambda h: (0, h)),
            column(lambda h: (0, heads)),
            column(lambda h: (0, heads + 1)),
            pl.BlockSpec((1, HEAD_SIZE), whole),
            pl.BlockSpec((1, HEAD_SIZE), whole),
            column(whole),
            column(whole),
        ],
        out_specs=[
            column(lambda h: (0, h)),
            pl.BlockSpec((1, 1, span), lambda h: (h, 0, 0)),
            column(lambda h: (0, h)),
        ],
        out_shape=[
            jax.ShapeDtypeStruct((span, heads * HEAD_SIZE), BF16),
            jax.ShapeDtypeStruct((heads, 1, span), F32),
            jax.ShapeDtypeStruct((span, heads * HEAD_SIZE), BF16),
        ],
        scratch_shapes=[
            pltpu.VMEM((span, HEAD_SIZE), BF16),
            pltpu.VMEM((HEAD_SIZE, span), BF16),
        ],
        cost_estimate=pl.CostEstimate(
            flops=4 * heads * keys * HEAD_SIZE,
            bytes_accessed=span * HEAD_SIZE * (8 * heads + 16),
            transcendentals=heads * keys,
        ),
        compiler_params=pltpu.CompilerParams(vmem_limit_bytes=40 * 1024 * 1024),
        name="attend",
    )(prefix, qkv, qkv, qkv, qgain, kgain, cosine, sine)


def attend_back_kernel(
    prefix_ref, q_ref, k_ref, v_ref, qlow_ref, lse_ref, up_ref,
    qgain_ref, kgain_ref, cos_ref, sin_ref,
    dq_ref, dkv_ref, qterm_ref, kterm_ref,
    klow, kturned, vlow, dk, dv, dq,
):
    span = q_ref.shape[0]
    prefix = prefix_ref[0]
    head = pl.program_id(0)

    @pl.when(head == 0)
    def _():
        k = k_ref[...]
        low = rope(k * scale_of(k) * kgain_ref[...], cos_ref[...], sin_ref[...])
        klow[...] = low.astype(BF16)
        kturned[...] = low.T.astype(BF16)
        vlow[...] = v_ref[...].astype(BF16)
        dk[...] = jnp.zeros_like(dk)
        dv[...] = jnp.zeros_like(dv)
        qterm_ref[...] = jnp.zeros_like(qterm_ref)

    for at, rows, keys in block_spans(span):
        qlow = qlow_ref[at : at + rows, :]
        up = up_ref[at : at + rows, :]
        scores = dot(klow[:keys, :], qlow, ((1,), (1,))) * SCALE
        allowed = allowed_of(at, rows, keys, prefix)
        weights = jnp.where(allowed, jnp.exp(scores - lse_ref[0, :, at : at + rows]), 0.0)
        weight_grad = dot(vlow[:keys, :], up, ((1,), (1,)))
        delta = jnp.sum(weights * weight_grad, axis=0, keepdims=True)
        score_grad = (weights * (weight_grad - delta)).astype(BF16)
        dv[:keys, :] += dot(weights.astype(BF16), up)
        dk[:keys, :] += dot(score_grad, qlow)
        dq[at : at + rows, :] = dot(kturned[:, :keys], score_grad).T

    q = q_ref[...]
    scaling = scale_of(q)
    unit = q * scaling
    turned = rope_back(dq[...] * SCALE, cos_ref[...], sin_ref[...])
    qterm_ref[...] += jnp.sum(turned * unit, axis=0, keepdims=True)
    dq_ref[...] = norm_back(turned, unit, scaling, qgain_ref[...]).astype(BF16)

    @pl.when(head == pl.num_programs(0) - 1)
    def _():
        k = k_ref[...]
        unit = k * scale_of(k)
        turned = rope_back(dk[...] * SCALE, cos_ref[...], sin_ref[...])
        kterm_ref[...] = jnp.sum(turned * unit, axis=0, keepdims=True)
        dkv_ref[:, :HEAD_SIZE] = turned.astype(BF16)
        dkv_ref[:, HEAD_SIZE:] = dv[...].astype(BF16)


def attend_back(prefix, qkv, heads, qlow, lse, upstream, qgain, kgain, cosine, sine):
    span = qkv.shape[0]
    whole = lambda h: (0, 0)
    column = lambda index: pl.BlockSpec((span, HEAD_SIZE), index)
    row = pl.BlockSpec((1, HEAD_SIZE), whole)
    keys = sum(rows * keys for _, rows, keys in block_spans(span))
    return pl.pallas_call(
        attend_back_kernel,
        grid=(heads,),
        in_specs=[
            pl.BlockSpec(memory_space=pltpu.SMEM),
            column(lambda h: (0, h)),
            column(lambda h: (0, heads)),
            column(lambda h: (0, heads + 1)),
            column(lambda h: (0, h)),
            pl.BlockSpec((1, 1, span), lambda h: (h, 0, 0)),
            column(lambda h: (0, h)),
            row,
            row,
            column(whole),
            column(whole),
        ],
        out_specs=[
            column(lambda h: (0, h)),
            pl.BlockSpec((span, 2 * HEAD_SIZE), whole),
            row,
            row,
        ],
        out_shape=[
            jax.ShapeDtypeStruct((span, heads * HEAD_SIZE), BF16),
            jax.ShapeDtypeStruct((span, 2 * HEAD_SIZE), BF16),
            jax.ShapeDtypeStruct((1, HEAD_SIZE), F32),
            jax.ShapeDtypeStruct((1, HEAD_SIZE), F32),
        ],
        scratch_shapes=[
            pltpu.VMEM((span, HEAD_SIZE), BF16),
            pltpu.VMEM((HEAD_SIZE, span), BF16),
            pltpu.VMEM((span, HEAD_SIZE), BF16),
            pltpu.VMEM((span, HEAD_SIZE), F32),
            pltpu.VMEM((span, HEAD_SIZE), F32),
            pltpu.VMEM((span, HEAD_SIZE), F32),
        ],
        cost_estimate=pl.CostEstimate(
            flops=10 * heads * keys * HEAD_SIZE,
            bytes_accessed=span * HEAD_SIZE * (10 * heads + 16),
            transcendentals=heads * keys,
        ),
        compiler_params=pltpu.CompilerParams(vmem_limit_bytes=48 * 1024 * 1024),
        name="attend_back",
    )(prefix, qkv, qkv, qkv, qlow, lse, upstream, qgain, kgain, cosine, sine)


def exchange(x, axes):
    return lax.all_to_all(x, axes, split_axis=0, concat_axis=0, tiled=True)


def shards(
    tokens,
    routes,
    prefix_len,
    query_weight,
    key_matrix,
    value_matrix,
    out_weight,
    router_weight,
    attention_gain,
    mixture_gain,
    query_gain,
    key_norm_gain,
    expert_gate,
    expert_up,
    expert_down,
    cotangent,
):
    planes = lax.axis_size("dp")
    lanes = lax.axis_size("expert")
    plane = lax.axis_index("dp")
    lane = lax.axis_index("expert")
    devices = planes * lanes
    resident, width = tokens.shape
    span = lanes * resident
    group = planes * resident
    columns = query_weight.shape[1]
    heads = columns // HEAD_SIZE
    narrow = key_matrix.shape[1]
    sharers = lanes // KEY_VALUE_HEADS
    member = lane % sharers
    experts = router_weight.shape[1] * lanes
    own_expert = plane * lanes + lane
    slots = planes * max(2, 6 * resident * TOP // (5 * experts))

    def to_all(x):
        return exchange(jnp.broadcast_to(x[None], (devices,) + x.shape), BOTH)

    def from_member(x, step):
        pairs = [(i, i - i % sharers + (i + step) % sharers) for i in range(lanes)]
        return lax.ppermute(x, "expert", pairs)

    residual = tokens.astype(F32)
    scaling_in = scale_of(residual)
    unit_in = residual * scaling_in
    normed = lax.all_gather(
        (unit_in * attention_gain).astype(BF16), "expert", axis=0, tiled=True
    )

    projection = lax.all_gather(
        jnp.concatenate([query_weight, key_matrix, value_matrix], axis=1), "dp", axis=0, tiled=True
    )
    turns = [projection[:, columns:]]
    turns += [from_member(turns[0], step) for step in range(1, sharers)]
    ordered = []
    for place in range(sharers):
        step_of = (member - place) % sharers
        piece = turns[0]
        for step in range(1, sharers):
            piece = jnp.where(step_of == step, turns[step], piece)
        ordered.append(piece)
    wide = jnp.concatenate(
        [projection[:, :columns]]
        + [piece[:, :narrow] for piece in ordered]
        + [piece[:, narrow:] for piece in ordered],
        axis=1,
    )
    out_rows = lax.all_gather(out_weight, "dp", axis=0, tiled=True)
    out_rows = lax.all_to_all(
        out_rows.reshape(lanes, columns, out_weight.shape[1]),
        "expert", split_axis=0, concat_axis=2, tiled=True,
    ).reshape(columns, width)

    expert_ids = jnp.arange(experts, dtype=jnp.int32)
    mask_turned = jnp.sum(
        (routes.T[:, None, :] == expert_ids[None, :, None]).astype(F32), axis=0
    )
    mask = mask_turned.T
    masks = to_all(mask_turned.astype(BF16)).reshape(planes, lanes, experts, resident)
    earlier = (
        lax.broadcasted_iota(jnp.int32, (group, group), 0)
        < lax.broadcasted_iota(jnp.int32, (group, group), 1)
    ).astype(BF16)
    slot_ids = lax.broadcasted_iota(jnp.int32, (1, slots, 1), 1)

    def slot_table(chosen):
        rank = dot(chosen, earlier).astype(jnp.int32)
        rank = jnp.where(chosen > 0, rank, -1)
        return (rank[:, None, :] == slot_ids).astype(BF16)

    send_mask = lax.dynamic_slice_in_dim(
        lax.dynamic_index_in_dim(masks, lane, 1, keepdims=False), plane * lanes, lanes, 1
    )
    send_table = slot_table(send_mask.transpose(1, 0, 2).reshape(lanes, group))
    send_rows = send_table.reshape(lanes * slots, group)
    here_mask = lax.dynamic_index_in_dim(masks, own_expert, 2, keepdims=False)
    here_table = slot_table(here_mask.transpose(1, 0, 2).reshape(lanes, group))
    row_mask = jnp.einsum(
        "lspr,plxr->lsx",
        here_table.reshape(lanes, slots, planes, resident),
        masks,
        preferred_element_type=F32,
    ).reshape(lanes * slots, experts)
    router_turned = (
        to_all(router_weight.T)
        .reshape(planes, lanes, experts // lanes, width // planes)
        .transpose(1, 2, 0, 3)
        .reshape(experts, width)
    )

    def dispatch(rows):
        gathered = lax.all_gather(rows, "dp", axis=0, tiled=True)
        placed = dot(send_rows, gathered).astype(BF16)
        return exchange(placed.reshape(lanes, slots, width), "expert").reshape(
            lanes * slots, width
        )

    def collect(rows):
        arrived = exchange(rows.reshape(lanes, slots, width), "expert")
        summed = dot(send_rows, arrived.reshape(lanes * slots, width), ((0,), (0,)))
        return lax.psum_scatter(
            summed.astype(BF16), "dp", scatter_dimension=0, tiled=True
        ).astype(F32)

    upstream_rows = dispatch(cotangent)

    prefix = prefix_len.astype(jnp.int32)
    cosine, sine = rotary_tables(span)
    qgain, kgain = query_gain[None, :], key_norm_gain[None, :]
    qkv = dot(normed, wide)
    attended, lse, qlow = attend(prefix, qkv, heads, qgain, kgain, cosine, sine)
    mixed_out = lax.psum_scatter(
        dot(attended, out_rows).astype(BF16), "expert", scatter_dimension=0, tiled=True
    )
    after_attn = residual + mixed_out.astype(F32)
    scaling_mix = scale_of(after_attn)
    unit_mix = after_attn * scaling_mix
    mixed_low = (unit_mix * mixture_gain).astype(BF16)

    rows = dispatch(mixed_low)

    def chosen_softmax(logits, chosen):
        logits = jnp.where(chosen > 0, logits, VERY_NEGATIVE)
        high = jnp.max(logits, axis=-1, keepdims=True)
        weights = jnp.where(chosen > 0, jnp.exp(logits - high), 0.0)
        return weights / jnp.maximum(jnp.sum(weights, axis=-1, keepdims=True), 1e-30)

    row_weights = chosen_softmax(dot(rows, router_turned, ((1,), (1,))), row_mask)
    row_weight = jnp.sum(
        jnp.where(expert_ids[None, :] == own_expert, row_weights, 0.0), axis=-1, keepdims=True
    )
    gate_matrix, up_matrix, down_matrix = expert_gate[0], expert_up[0], expert_down[0]
    gate_raw = dot(rows, gate_matrix)
    up_raw = dot(rows, up_matrix)
    gate_sig = jax.nn.sigmoid(gate_raw)
    activated = (gate_raw * gate_sig * up_raw).astype(BF16)
    produced_grad = (row_weight * upstream_rows.astype(F32)).astype(BF16)
    activated_grad = dot(produced_grad, down_matrix, ((1,), (1,)))
    gate_grad = (activated_grad * up_raw * gate_sig * (1.0 + gate_raw * (1.0 - gate_sig))).astype(
        BF16
    )
    up_grad = (activated_grad * gate_raw * gate_sig).astype(BF16)
    row_grad = (
        dot(gate_grad, gate_matrix, ((1,), (1,))) + dot(up_grad, up_matrix, ((1,), (1,)))
    ).astype(BF16)
    rows_back = collect(row_grad)

    produced = dot(activated, down_matrix).astype(BF16).astype(F32)
    route_rows = jnp.sum(produced * upstream_rows.astype(F32), axis=-1)
    route_dense = jnp.sum(
        here_table.astype(F32) * route_rows.reshape(lanes, slots)[:, :, None], axis=1
    )
    route_grad = exchange(
        route_dense.reshape(lanes, planes, resident).transpose(1, 0, 2).reshape(devices, resident),
        BOTH,
    ).T
    down_gradient = dot(activated, produced_grad, ((0,), (0,)))
    gate_gradient = dot(rows, gate_grad, ((0,), (0,)))
    up_gradient = dot(rows, up_grad, ((0,), (0,)))
    mixture = collect((row_weight * produced).astype(BF16))
    layer_out = (after_attn + mixture).astype(BF16)

    weight = chosen_softmax(dot(mixed_low, router_turned, ((1,), (1,))), mask)
    logit_grad = (
        weight * (route_grad - jnp.sum(weight * route_grad, axis=-1, keepdims=True))
    ).astype(BF16)
    upstream = cotangent.astype(F32)
    mixed_grad = dot(logit_grad, router_turned) + rows_back
    mixture_terms = jnp.sum(mixed_grad * unit_mix, axis=0)
    after_grad = upstream + norm_back(mixed_grad, unit_mix, scaling_mix, mixture_gain)
    after_low = lax.all_gather(after_grad.astype(BF16), "expert", axis=0, tiled=True)

    attended_grad = dot(after_low, out_rows, ((1,), (1,))).astype(BF16)
    dq, dkv, qterm, kterm = attend_back(
        prefix, qkv, heads, qlow, lse, attended_grad, qgain, kgain, cosine, sine
    )
    dkv_sum = dkv.astype(F32)
    for step in range(1, sharers):
        dkv_sum = dkv_sum + from_member(dkv, step).astype(F32)
    key_raw = qkv[:, columns : columns + HEAD_SIZE]
    scaling_key = scale_of(key_raw)
    key_back = norm_back(
        dkv_sum[:, :HEAD_SIZE], key_raw * scaling_key, scaling_key, kgain
    ).astype(BF16)
    value_back = dkv_sum[:, HEAD_SIZE:].astype(BF16)

    def own_columns(x):
        own = x[:, :narrow]
        for place in range(1, sharers):
            own = jnp.where(member == place, x[:, place * narrow : (place + 1) * narrow], own)
        return own

    back = jnp.concatenate([dq, own_columns(key_back), own_columns(value_back)], axis=1)
    normed_part = dot(back, projection, ((1,), (1,)))
    attention_terms = jnp.sum(normed_part * normed.astype(F32), axis=0) / attention_gain
    normed_grad = lax.psum_scatter(
        normed_part.astype(BF16), "expert", scatter_dimension=0, tiled=True
    ).astype(F32)
    input_grad = after_grad + norm_back(normed_grad, unit_in, scaling_in, attention_gain)

    projection_share = lax.psum_scatter(
        dot(normed, back, ((0,), (0,))).astype(BF16), "dp", scatter_dimension=0, tiled=True
    ).astype(F32)
    out_part = dot(attended, after_low, ((0,), (0,))).astype(BF16)
    out_part = lax.all_to_all(
        out_part.reshape(1, columns, width), "expert", split_axis=2, concat_axis=0, tiled=True
    ).reshape(lanes * columns, width // lanes)
    out_share = lax.psum_scatter(out_part, "dp", scatter_dimension=0, tiled=True).astype(F32)
    router_part = dot(logit_grad, mixed_low, ((0,), (0,))).astype(BF16)
    router_part = exchange(
        router_part.reshape(lanes, experts // lanes, planes, width // planes)
        .transpose(2, 0, 1, 3)
        .reshape(devices, experts // lanes, width // planes),
        BOTH,
    )
    router_share = jnp.sum(router_part.astype(F32), axis=0).T

    terms = jnp.concatenate([attention_terms, mixture_terms, qterm[0], kterm[0]]).reshape(
        -1, HEAD_SIZE
    )
    totals = jnp.sum(to_all(terms), axis=0).reshape(-1)
    return (
        layer_out,
        input_grad,
        projection_share[:, :columns],
        projection_share[:, columns : columns + narrow],
        projection_share[:, columns + narrow :],
        out_share,
        router_share,
        totals[:width],
        totals[width : 2 * width],
        totals[2 * width : 2 * width + HEAD_SIZE],
        totals[2 * width + HEAD_SIZE :],
        gate_gradient[None],
        up_gradient[None],
        down_gradient[None],
    )


def solution(mesh):
    rows = P(BOTH, None)
    block = P("dp", "expert")
    stack = P(BOTH, None, None)
    in_specs = (
        rows, rows, P("dp"), block, block, block, block, block,
        P(), P(), P(), P(), stack, stack, stack, rows,
    )
    out_specs = (
        rows, rows, block, block, block, block, block,
        P(), P(), P(), P(), stack, stack, stack,
    )
    return jax.shard_map(shards, mesh=mesh, in_specs=in_specs, out_specs=out_specs, check_vma=False)
```
